32 devices in a mesh: wide: 8 (over z, x), eight: 4 (over y, core).
Axes of the slice: x: 2, y: 2, z: 4, core: 2. Of those that a mesh axis runs over, the one named last changes fastest.
Arguments:
- start_vectors: bfloat16 [128, 96, 4096], P('wide', 'eight'), may hold values from -6 to 6
- conductance: float32 [128, 4096], P('wide'), may hold values from 1 to 100
- counts: int32 [128], P('wide'), may hold values from 1 to 96, as said below
- element_of: int32 [128, 8], P('wide'), may hold values from 0 to 127, as said below
- capacity: float32 [128, 512], P(('wide', 'eight')), may hold values from 0.25 to 4
- coarse_in: float32 [128, 96, 64], P(('wide', 'eight')), may hold values from -6 to 6
Outputs:
- galerkin: float32 [128, 768, 768], P(('wide', 'eight'))
- coarse_out: float32 [128, 96, 64], P(('wide', 'eight'))
The draws below stay inside these ranges and needn't reach their ends.
Inputs may be any that keep to these rules, and one draw needn't show every extreme that they name: `counts`: some neighbourhood keeps exactly 96 basis functions. For each octant o, element_of[:, o] names every element exactly once. Element e belongs to device e // 4 in the order of wide+eight, and the 16 neighbourhoods of each index of wide name, over all their octants, exactly 4 elements of each device.
All inputs are finite; a program needn't handle non-finite values.
Results may differ from the reference program's by a relative error of at most 0.0004.
Values sent between devices are 32-bit elements; how exact they have to be, the bound alone decides.
No kernel may reach another device: no remote copies, remote signals or barrier semaphores. Data moves between devices by JAX's collectives and lax.ppermute only.
A program may use at most 192 MiB of HBM per device.

```python
import math
import jax
import jax.numpy as jnp
from jax import lax

SIDE = 16
SLOTS = 96
VECS = 64
PASSES = 6
NBH_DEV = 16
CELLS = 4096
ECELLS = 512
NBH = 128
ELEMS = 128
N_WIDE = 8
N_EIGHT = 4


def draw_counts(key, part):
    key_base = jax.random.fold_in(key, 3)
    first_key, second_key, third_key = jax.random.split(key_base, 3)
    first_draw = jax.random.randint(first_key, (NBH,), 1, SLOTS + 1)
    second_draw = jax.random.randint(second_key, (NBH,), 1, SLOTS + 1)
    fullest = jax.random.randint(third_key, (), 0, NBH)
    kept = jnp.minimum(first_draw, second_draw)
    kept = jnp.where(jnp.arange(NBH) == fullest, SLOTS, kept)
    return kept.astype(jnp.int32)


def incidence(key):
    devices = N_WIDE * N_EIGHT
    key_base = jax.random.fold_in(key, 11)
    shuffle_key, relabel_key, tie_key = jax.random.split(key_base, 3)
    wide_index = jnp.arange(N_WIDE, dtype=jnp.int32)[:, None, None]
    octant_index = jnp.arange(8, dtype=jnp.int32)[None, :, None]
    member_index = jnp.arange(NBH_DEV, dtype=jnp.int32)[None, None, :]
    base_dest = (member_index + NBH_DEV * octant_index + N_EIGHT * wide_index) % devices
    base_dest = jnp.broadcast_to(base_dest, (N_WIDE, 8, NBH_DEV))
    shuffle_keys = jax.random.split(shuffle_key, N_WIDE * 8)
    shuffles = jax.vmap(lambda one_key: jax.random.permutation(one_key, NBH_DEV))(shuffle_keys)
    shuffles = shuffles.reshape(N_WIDE, 8, NBH_DEV).astype(jnp.int32)
    base_dest = jnp.take_along_axis(base_dest, shuffles, axis=2)
    relabel = jax.random.permutation(relabel_key, devices).astype(jnp.int32)
    dest_dev = relabel[base_dest]
    dest_by_octant = jnp.transpose(dest_dev, (1, 0, 2)).reshape(8, N_WIDE * NBH_DEV)
    tie_keys = jax.random.split(tie_key, 8)
    tie_break = jax.vmap(lambda one_key: jax.random.permutation(one_key, N_WIDE * NBH_DEV))(tie_keys).astype(jnp.int32)
    score = dest_by_octant * (N_WIDE * NBH_DEV) + tie_break
    ordering = jnp.argsort(score, axis=1)
    element_ids = jnp.argsort(ordering, axis=1)
    return jnp.transpose(element_ids).astype(jnp.int32)


def draw_element_of(key, part):
    return incidence(key)


def steps_of(own_key, shape, cuts, smallest, high):
    def one(axis_at, blocks):
        steps = jax.random.uniform(jax.random.fold_in(jax.random.fold_in(own_key, 6), axis_at), (blocks,), jnp.float32, smallest / len(cuts), high / len(cuts))
        return jnp.repeat(jnp.exp(steps), shape[axis_at] // blocks).reshape((-1,) + (1,) * (len(shape) - axis_at - 1))

    factor_of = one(*cuts[0])
    for cut in cuts[1:]:
        factor_of = factor_of * one(*cut)
    return factor_of


def centred(stream_key, extent, width, reach, cuts=(), kind=jnp.bfloat16):
    array = jax.random.normal(stream_key, extent, jnp.float32) * width
    if len(cuts) > 0:
        array = steps_of(stream_key, extent, cuts, -0.22, 0.18) * array
    return jnp.clip(array, min=-reach, max=reach).astype(kind)


def setup_inputs(seed: int = 0) -> dict:
    arg_keys = jax.random.split(jax.random.key(seed), 7)
    return {
        "start_vectors": centred(arg_keys[0], (NBH, SLOTS, CELLS), 1.0, 6.0, ((0, 8), (1, 4))),
        "conductance": jnp.clip(jnp.exp(math.log(100.0) - 4.6051702 * jax.random.uniform(arg_keys[1], (NBH, CELLS), jnp.float32) ** steps_of(arg_keys[1], (NBH, CELLS), ((0, 8),), -0.2, 0.2)), 1.0, 100.0),
        "counts": draw_counts(jax.random.fold_in(arg_keys[6], 71), 0),
        "element_of": draw_element_of(jax.random.fold_in(arg_keys[6], 71), 0),
        "capacity": jnp.clip(jnp.exp(math.log(4.0) - 2.7725887 * jax.random.uniform(arg_keys[4], (ELEMS, ECELLS), jnp.float32) ** steps_of(arg_keys[4], (ELEMS, ECELLS), ((0, 32),), -0.2, 0.2)), 0.25, 4.0),
        "coarse_in": centred(arg_keys[5], (NBH, SLOTS, VECS), 1.0, 6.0, ((0, 32),), jnp.float32),
    }


def stencil_weights(conductance, edge_cells):
    cubic_cells = conductance.reshape(conductance.shape[:-1] + (edge_cells, edge_cells, edge_cells))
    leading = cubic_cells.ndim - 3
    padded = jnp.pad(cubic_cells, [(0, 0)] * leading + [(1, 1)] * 3, mode='edge')
    diagonal = jnp.zeros_like(cubic_cells)
    neighbour_links = []
    strides = (edge_cells * edge_cells, edge_cells, 1)
    for direction in range(3):
        position = lax.broadcasted_iota(jnp.int32, cubic_cells.shape, leading + direction)
        for toward in (-1, 1):
            starts = [0] * leading + [1, 1, 1]
            starts[leading + direction] = 1 + toward
            limits = [starts[dim_index] + cubic_cells.shape[dim_index] for dim_index in range(cubic_cells.ndim)]
            beside = lax.slice(padded, starts, limits)
            face_weight = 0.5 * (cubic_cells + beside)
            diagonal = diagonal + face_weight
            inside = (position + toward >= 0) & (position + toward < edge_cells)
            linked = jnp.where(inside, face_weight, jnp.zeros_like(face_weight))
            neighbour_links.append((toward * strides[direction], linked.reshape(conductance.shape)))
    return (diagonal.reshape(conductance.shape), neighbour_links)

def operate(field, diagonal, neighbour_links, plane_span):
    cell_total = field.shape[-1]
    padded = jnp.pad(field, [(0, 0)] * (field.ndim - 1) + [(plane_span, plane_span)])
    result = diagonal * field
    for offset, linked in neighbour_links:
        moved = lax.slice_in_dim(padded, plane_span + offset, plane_span + offset + cell_total, axis=field.ndim - 1)
        result = result - linked * moved
    return result

def hat_bump(edge_cells):
    half_side = edge_cells // 2
    along = (jnp.arange(edge_cells, dtype=jnp.float32) + 0.5) / half_side
    rising = jnp.minimum(along, 2.0 - along)
    return (rising[:, None, None] * rising[None, :, None] * rising[None, None, :]).reshape(-1)

def filtered_basis(start, conductance, live, edge_cells, sweeps):
    diagonal, neighbour_links = stencil_weights(conductance, edge_cells)
    upper_bound = 2.0 * lax.optimization_barrier(jnp.max(diagonal, axis=-1))
    centre = (0.5625 * upper_bound)[..., None, None]
    radius = (0.4375 * upper_bound)[..., None, None]
    diagonal = diagonal[..., None, :]
    neighbour_links = [(offset, linked[..., None, :]) for offset, linked in neighbour_links]
    plane_span = edge_cells * edge_cells
    previous = start
    current = (operate(previous, diagonal, neighbour_links, plane_span) - centre * previous) / radius
    for repeat in range(sweeps - 1):
        previous, current = (current, 2.0 * (operate(current, diagonal, neighbour_links, plane_span) - centre * current) / radius - previous)
    norm_scale = lax.rsqrt(lax.optimization_barrier(jnp.mean(current * current, axis=-1, keepdims=True)) + 1e-05)
    return current * norm_scale * hat_bump(edge_cells) * live[..., None]

def octant_pieces(basis, edge_cells):
    half_side = edge_cells // 2
    leading = basis.shape[:-1]
    rank_lead = len(leading)
    cubic = basis.reshape(leading + (2, half_side, 2, half_side, 2, half_side))
    axes_order = tuple(range(rank_lead - 1)) + (rank_lead, rank_lead + 2, rank_lead + 4, rank_lead - 1, rank_lead + 1, rank_lead + 3, rank_lead + 5)
    cubic = jnp.transpose(cubic, axes_order)
    return cubic.reshape(leading[:-1] + (8, leading[-1], half_side * half_side * half_side))

def reference(start_vectors, conductance, counts, element_of, capacity, coarse_in):
    slot_ids = jnp.arange(SLOTS, dtype=jnp.int32)

    def one_hood(packed):
        start, local_cond, count = packed
        live = (slot_ids < count).astype(jnp.float32)
        basis = filtered_basis(start.astype(jnp.float32), local_cond, live, SIDE, PASSES)
        return octant_pieces(basis, SIDE)
    pieces = lax.map(one_hood, (start_vectors, conductance, counts))
    octants = jnp.arange(8, dtype=jnp.int32)
    contributor = jnp.zeros((ELEMS, 8), jnp.int32).at[element_of, octants[None, :]].set(jnp.arange(NBH, dtype=jnp.int32)[:, None])

    def one_element(packed):
        hoods, weight = packed
        gathered = pieces[hoods, octants].reshape(8 * SLOTS, ECELLS)
        galerkin = jnp.dot(gathered * weight[None, :], gathered.T, precision=lax.Precision.HIGHEST) / ECELLS
        coarse_rows = coarse_in[hoods].reshape(8 * SLOTS, VECS)
        applied = jnp.dot(galerkin, coarse_rows, precision=lax.Precision.HIGHEST)
        return (galerkin, applied.reshape(8, SLOTS, VECS))
    galerkin, applied = lax.map(one_element, (contributor, capacity))
    coarse_out = jnp.zeros((NBH, SLOTS, VECS), jnp.float32).at[contributor].add(applied)
    return (galerkin, coarse_out)
```

```python
import functools

import jax
import jax.numpy as jnp
from jax import lax
from jax.experimental import pallas as pl
from jax.experimental.pallas import tpu as pltpu
from jax.sharding import PartitionSpec as P

SIDE = 16
PASSES = 6
ECELLS = 512
LANES = 128
ROWS = 8
HALF = SIDE // 2
TILES = SIDE * SIDE * SIDE // LANES
PAIR = SIDE * SIDE // LANES

ANY = pl.BlockSpec(memory_space=pl.ANY)
VMEM = pl.BlockSpec(memory_space=pltpu.VMEM)
SMEM = pl.BlockSpec(memory_space=pltpu.SMEM)


def hat(i):
    return min(i + 0.5, SIDE - 0.5 - i) / HALF


def stencil_table(cond, w_ref):
    cells = cond.shape[1]
    at = lax.broadcasted_iota(jnp.int32, cond.shape, 1)
    diagonal = jnp.zeros_like(cond)
    links = []
    for stride in (SIDE * SIDE, SIDE, 1):
        position = (at // stride) % SIDE
        for toward in (-1, 1):
            beside = pltpu.roll(cond, (-toward * stride) % cells, 1)
            inside = (position + toward >= 0) & (position + toward < SIDE)
            face = 0.5 * (cond + jnp.where(inside, beside, cond))
            diagonal = diagonal + face
            links.append(jnp.where(inside, face, 0.0))
    upper = 2.0 * jnp.max(diagonal, axis=1, keepdims=True)
    twice = 2.0 / (0.4375 * upper)
    table = [(diagonal - 0.5625 * upper) * twice] + [link * twice for link in links]
    for i, values in enumerate(table):
        for t in range(TILES):
            w_ref[i, t] = values[:, t * LANES : (t + 1) * LANES]


def filter_kernel(first_slot, groups, target_ref, counts_ref, sv_ref, cond_ref, send_ref, w_ref, y_ref, out_ref, sems):
    n = pl.program_id(0)
    last = pl.num_programs(0) - 1
    rows = groups * ROWS
    lane = lax.broadcasted_iota(jnp.int32, (ROWS, LANES), 1)
    low_row = lane < SIDE
    high_row = lane >= LANES - SIDE

    @pl.when(n == 0)
    def _():
        stencil_table(cond_ref[...], w_ref)

    def weight(k, t):
        return w_ref[k, t, pl.ds(n, ROWS, 0), :]

    start = sv_ref[0].astype(jnp.float32)
    for g in range(groups):
        y_ref[0, g] = start[first_slot + g * ROWS : first_slot + (g + 1) * ROWS, :]

    squares = [jnp.zeros((ROWS, LANES), jnp.float32) for _ in range(groups)]
    for sweep in range(PASSES):
        src, dst, old = sweep % 3, (sweep + 1) % 3, (sweep + 2) % 3

        def tile(g, a, d):
            t = a * PAIR + d
            return y_ref[src, g, :, t * LANES : (t + 1) * LANES]

        window = [[None] + [[tile(g, a, d) for d in range(PAIR)] for a in range(1)] for g in range(groups)]
        for a in range(SIDE):
            ups = []
            for g in range(groups):
                below, here = window[g]
                above = [tile(g, a + 1, d) for d in range(PAIR)] if a + 1 < SIDE else None
                ups.append((below, here, above))
                window[g] = [here, above]
            back = [[pltpu.roll(u[1][d], SIDE, 1) for d in range(PAIR)] for u in ups]
            fore = [[pltpu.roll(u[1][d], LANES - SIDE, 1) for d in range(PAIR)] for u in ups]
            for d in range(PAIR):
                t = a * PAIR + d
                w = [weight(k, t) for k in range(7)]
                for g in range(groups):
                    below, here, above = ups[g]
                    value = w[0] * here[d]
                    if below is not None:
                        value = value - w[1] * below[d]
                    if above is not None:
                        value = value - w[2] * above[d]
                    lower = back[g][d] if d == 0 else jnp.where(low_row, back[g][d - 1], back[g][d])
                    upper = fore[g][d] if d == PAIR - 1 else jnp.where(high_row, fore[g][d + 1], fore[g][d])
                    value = value - w[3] * lower
                    value = value - w[4] * upper
                    value = value - w[5] * pltpu.roll(here[d], 1, 1)
                    value = value - w[6] * pltpu.roll(here[d], LANES - 1, 1)
                    if sweep == 0:
                        value = 0.5 * value
                    else:
                        value = value - y_ref[old, g, :, t * LANES : (t + 1) * LANES]
                    y_ref[dst, g, :, t * LANES : (t + 1) * LANES] = value
                    if sweep == PASSES - 1:
                        squares[g] = squares[g] + value * value
    final = PASSES % 3

    slot = lax.rem(n, 2)

    def copy_out(step_slot, piece, o):
        return pltpu.make_async_copy(out_ref.at[step_slot, o], send_ref.at[piece], sems.at[step_slot, o])

    @pl.when(n >= 2)
    def _():
        for o in range(8):
            copy_out(slot, 0, o).wait()

    column = lax.rem(lax.div(lane, SIDE), HALF)
    across = (lax.rem(lane, SIDE)).astype(jnp.float32)
    hat_c = jnp.minimum(across + 0.5, SIDE - 0.5 - across) / HALF
    even = lax.rem(lax.div(lane, HALF), 2) == 0
    bumps = []
    for d in range(PAIR):
        along = (column + d * HALF).astype(jnp.float32)
        bumps.append(hat_c * (jnp.minimum(along + 0.5, SIDE - 0.5 - along) / HALF))
    base = lax.axis_index("eight") * sv_ref.shape[1] + first_slot
    for g in range(groups):
        mean = jnp.sum(squares[g], axis=1, keepdims=True) / (TILES * LANES)
        row = lax.broadcasted_iota(jnp.int32, (ROWS, 1), 0) + (base + g * ROWS)
        scale = lax.rsqrt(mean + 1e-05) * (row < counts_ref[n]).astype(jnp.float32)
        for d in range(PAIR):
            weight_d = scale * bumps[d]
            for dx in range(2):
                for p in range(HALF // 2):
                    pair = []
                    for h in range(2):
                        a = dx * HALF + h * (HALF // 2) + p
                        t = a * PAIR + d
                        pair.append(y_ref[final, g, :, t * LANES : (t + 1) * LANES] * (weight_d * hat(a)))
                    near = jnp.where(even, pair[0], pltpu.roll(pair[1], HALF, 1))
                    far = jnp.where(even, pltpu.roll(pair[0], LANES - HALF, 1), pair[1])
                    for dz, value in enumerate((near, far)):
                        out_ref[slot, dx * 4 + d * 2 + dz, g * ROWS : (g + 1) * ROWS, p * LANES : (p + 1) * LANES] = value
    for o in range(8):
        copy_out(slot, target_ref[n * 8 + o], o).start()

    @pl.when(n == last)
    def _():
        for o in range(8):
            copy_out(1 - slot, 0, o).wait()
        for o in range(8):
            copy_out(slot, 0, o).wait()


def filter_call(first_slot, groups, target, counts, start_vectors, conductance):
    hoods, width, cells = start_vectors.shape
    rows = groups * ROWS
    return pl.pallas_call(
        functools.partial(filter_kernel, first_slot, groups),
        grid_spec=pltpu.PrefetchScalarGridSpec(
            num_scalar_prefetch=2,
            grid=(hoods,),
            in_specs=[
                pl.BlockSpec((1, width, cells), lambda n, t, c: (n, 0, 0)),
                pl.BlockSpec((hoods, cells), lambda n, t, c: (0, 0)),
            ],
            out_specs=ANY,
            scratch_shapes=[
                pltpu.VMEM((7, TILES, hoods, LANES), jnp.float32),
                pltpu.VMEM((3, groups, ROWS, cells), jnp.float32),
                pltpu.VMEM((2, 8, rows, ECELLS), jnp.float32),
                pltpu.SemaphoreType.DMA((2, 8)),
            ],
        ),
        out_shape=jax.ShapeDtypeStruct((hoods * 8, rows, ECELLS), jnp.float32),
        name="filter%d" % first_slot,
    )(target, counts, start_vectors, conductance)


def pack(blocks):
    if len(blocks) % 2:
        blocks = blocks + [jnp.zeros_like(blocks[0])]
    return [jnp.concatenate(blocks[i : i + 2], axis=1) for i in range(0, len(blocks), 2)]


def half(tile, k):
    vectors = LANES // 2
    return tile[:, (k % 2) * vectors : (k % 2 + 1) * vectors]


def packed_width(blocks):
    return (blocks + 1) // 2 * LANES


def coarse_pack_kernel(groups, in_ref, out_ref):
    owned, slots, _ = in_ref.shape
    width = slots // groups
    for e in range(groups):
        blocks = [
            in_ref[n, e * width + r : e * width + r + ROWS, :] for n in range(owned) for r in range(0, width, ROWS)
        ]
        for i, tile in enumerate(pack(blocks)):
            out_ref[e, :, i * LANES : (i + 1) * LANES] = tile


def rows_kernel(per_pair, target_ref, in_ref, out_ref, rows_ref, source_ref):
    groups = in_ref.shape[0]
    hoods, width, _ = rows_ref.shape
    owned = hoods // groups
    bits = width // ROWS
    for e in range(groups):
        for n in range(owned):
            for r in range(bits):
                k = n * bits + r
                rows_ref[e * owned + n, r * ROWS : (r + 1) * ROWS, :] = half(
                    in_ref[e, :, k // 2 * LANES : (k // 2 + 1) * LANES], k
                )

    def invert(p, carry):
        source_ref[target_ref[p]] = p
        return carry

    lax.fori_loop(0, hoods * 8, invert, 0)

    def place(d, carry):
        blocks = []
        for i in range(per_pair):
            n = lax.div(source_ref[d * per_pair + i], 8)
            blocks += [rows_ref[n, r * ROWS : (r + 1) * ROWS, :] for r in range(bits)]
        for i, tile in enumerate(pack(blocks)):
            out_ref[d, :, i * LANES : (i + 1) * LANES] = tile
        return carry

    lax.fori_loop(0, out_ref.shape[0], place, 0)


def sum_kernel(per_pair, target_ref, in_ref, out_ref, rows_ref, source_ref):
    groups = out_ref.shape[0]
    hoods, width, _ = rows_ref.shape
    owned = hoods // groups
    bits = width // ROWS
    rows_ref[...] = jnp.zeros_like(rows_ref)

    def invert(p, carry):
        source_ref[target_ref[p]] = p
        return carry

    lax.fori_loop(0, hoods * 8, invert, 0)

    def gather(d, carry):
        for i in range(per_pair):
            n = lax.div(source_ref[d * per_pair + i], 8)
            for r in range(bits):
                k = i * bits + r
                rows_ref[n, r * ROWS : (r + 1) * ROWS, :] += half(in_ref[d, :, k // 2 * LANES : (k // 2 + 1) * LANES], k)
        return carry

    lax.fori_loop(0, in_ref.shape[0], gather, 0)
    for e in range(groups):
        blocks = [
            rows_ref[e * owned + n, r * ROWS : (r + 1) * ROWS, :] for n in range(owned) for r in range(bits)
        ]
        for i, tile in enumerate(pack(blocks)):
            out_ref[e, :, i * LANES : (i + 1) * LANES] = tile


def coarse_out_kernel(in_ref, out_ref):
    groups = in_ref.shape[0]
    owned, slots, _ = out_ref.shape
    width = slots // groups
    bits = width // ROWS
    for e in range(groups):
        for n in range(owned):
            for r in range(bits):
                k = n * bits + r
                out_ref[n, e * width + r * ROWS : e * width + (r + 1) * ROWS, :] = half(
                    in_ref[e, :, k // 2 * LANES : (k // 2 + 1) * LANES], k
                )


def split(x):
    high = x.astype(jnp.bfloat16)
    return high, (x - high.astype(jnp.float32)).astype(jnp.bfloat16)


def product(x, y, dims):
    xh, xl = x
    yh, yl = y
    dot = functools.partial(lax.dot_general, dimension_numbers=(dims, ((), ())), preferred_element_type=jnp.float32)
    return dot(xh, yh) + (dot(xh, yl) + dot(xl, yh))


def gather_basis(chunks, groups, per_pair, ids_ref, got_refs, phi_ref, sems):
    width = sum(count for _, count in chunks) * ROWS
    stride = groups * width
    pieces = ids_ref.shape[0]

    def place(q, carry):
        row = ids_ref[q] * stride + lax.rem(lax.div(q, per_pair), groups) * width
        for k, (first, count) in enumerate(chunks):
            rows = count * ROWS
            pltpu.make_async_copy(
                got_refs[k].at[pl.ds(pl.multiple_of(q * rows, ROWS), rows)],
                phi_ref.at[pl.ds(pl.multiple_of(row + first, ROWS), rows)],
                sems.at[k],
            ).start()
        return carry

    lax.fori_loop(0, pieces, place, 0)
    for k, (first, count) in enumerate(chunks):
        pltpu.make_async_copy(got_refs[k], phi_ref.at[pl.ds(0, pieces * count * ROWS)], sems.at[k]).wait()


def applied_kernel(chunks, groups, per_pair, ids_ref, rows_in_ref, cap_ref, *refs):
    got_refs = refs[: len(chunks)]
    out_ref, phi_ref, r_ref, applied_ref, sems = refs[len(chunks) :]
    width = sum(count for _, count in chunks) * ROWS
    bits = width // ROWS
    stride = groups * width
    elements = cap_ref.shape[0]
    devices = rows_in_ref.shape[0]
    gather_basis(chunks, groups, per_pair, ids_ref, got_refs, phi_ref, sems)

    def row_of(s, i):
        return ids_ref[s * per_pair + i] * stride + lax.rem(s, groups) * width

    def place(s, carry):
        for i in range(per_pair):
            row = row_of(s, i)
            for r in range(bits):
                k = i * bits + r
                r_ref[pl.ds(pl.multiple_of(row + r * ROWS, ROWS), ROWS), :] = half(
                    rows_in_ref[s, :, k // 2 * LANES : (k // 2 + 1) * LANES], k
                )
        return carry

    lax.fori_loop(0, devices, place, 0)
    rows = 8 * stride
    for e in range(elements):
        phi = split(phi_ref[e * rows : (e + 1) * rows, :])
        r = split(jnp.transpose(r_ref[e * rows : (e + 1) * rows, :]))
        sums = product(r, phi, ((1,), (0,))) * cap_ref[e : e + 1, :]
        applied_ref[e * rows : (e + 1) * rows, :] = product(phi, split(sums), ((1,), (1,)))

    def back(s, carry):
        blocks = []
        for i in range(per_pair):
            row = row_of(s, i)
            blocks += [applied_ref[pl.ds(pl.multiple_of(row + r * ROWS, ROWS), ROWS), :] for r in range(bits)]
        for i, tile in enumerate(pack(blocks)):
            out_ref[s, :, i * LANES : (i + 1) * LANES] = tile
        return carry

    lax.fori_loop(0, devices, back, 0)


def galerkin_kernel(chunks, groups, per_pair, ids_ref, cap_ref, *refs):
    got_refs = refs[: len(chunks)]
    out_ref, phi_ref, sems = refs[len(chunks) :]
    width = sum(count for _, count in chunks) * ROWS
    rows = 8 * groups * width
    e = pl.program_id(0)

    @pl.when(e == 0)
    def _():
        gather_basis(chunks, groups, per_pair, ids_ref, got_refs, phi_ref, sems)

    phi = phi_ref[pl.ds(pl.multiple_of(e * rows, ROWS), rows), :]
    weighted = phi * cap_ref[pl.ds(e, 1), :]
    out_ref[0] = product(split(weighted), split(phi), ((1,), (1,)))


CHUNKS = ((0, 1), (8, 2))


def whole(f, shape, *args, scratch=(), prefetch=0, name=None):
    return pl.pallas_call(
        f,
        grid_spec=pltpu.PrefetchScalarGridSpec(
            num_scalar_prefetch=prefetch,
            grid=(),
            in_specs=[VMEM] * (len(args) - prefetch),
            out_specs=VMEM,
            scratch_shapes=list(scratch),
        ),
        out_shape=jax.ShapeDtypeStruct(shape, jnp.float32),
        name=name,
    )(*args)


def body(start_vectors, conductance, counts, element_of, capacity, coarse_in):
    groups = lax.axis_size("eight")
    devices = lax.axis_size("wide") * groups
    hoods, width, cells = start_vectors.shape
    owned = hoods // groups
    elements = capacity.shape[0]
    pieces = hoods * 8
    per_pair = pieces // devices
    slots, vectors = coarse_in.shape[1:]
    bits = width // ROWS
    chunks = CHUNKS
    both = ("wide", "eight")

    owner = (element_of // elements).reshape(-1)
    local = (element_of % elements * 8 + jnp.arange(8, dtype=jnp.int32)[None, :]).reshape(-1)
    order = jnp.arange(pieces, dtype=jnp.int32)
    earlier = (owner[:, None] == owner[None, :]) & (order[None, :] < order[:, None])
    target = owner * per_pair + jnp.sum(earlier.astype(jnp.int32), axis=1)

    got = []
    for at, count in chunks:
        send = filter_call(at, count, target, counts, start_vectors, conductance)
        if at == 0:
            coarse_in, local, target, send = lax.optimization_barrier((coarse_in, local, target, send))
        send = send.reshape(devices, per_pair, count * ROWS, ECELLS)
        arrived = lax.all_to_all(send, both, split_axis=0, concat_axis=0, tiled=True)
        got.append(arrived.reshape(pieces * count * ROWS, ECELLS))

    source = jnp.zeros(pieces, jnp.int32).at[target].set(local)
    ids = lax.all_to_all(source.reshape(devices, per_pair), both, split_axis=0, concat_axis=0, tiled=True).reshape(-1)

    near = packed_width(owned * bits)
    far = packed_width(per_pair * bits)
    out = whole(functools.partial(coarse_pack_kernel, groups), (groups, ROWS, near), coarse_in, name="coarse_pack")
    out = lax.all_to_all(out, "eight", split_axis=0, concat_axis=0, tiled=True)
    scratch = [pltpu.VMEM((hoods, width, vectors), jnp.float32), pltpu.SMEM((pieces,), jnp.int32)]
    out = whole(
        functools.partial(rows_kernel, per_pair),
        (devices, ROWS, far),
        target,
        out,
        scratch=scratch,
        prefetch=1,
        name="rows_out",
    )
    rows_in = lax.all_to_all(out, both, split_axis=0, concat_axis=0, tiled=True)

    cap = capacity.reshape(elements, 2, HALF // 2, HALF, HALF).transpose(0, 2, 3, 1, 4).reshape(elements, ECELLS) / ECELLS
    rows = 8 * slots
    phi = [pltpu.VMEM((elements * rows, ECELLS), jnp.float32)]
    sems = [pltpu.SemaphoreType.DMA((len(chunks),))]
    back = pl.pallas_call(
        functools.partial(applied_kernel, chunks, groups, per_pair),
        grid_spec=pltpu.PrefetchScalarGridSpec(
            num_scalar_prefetch=1,
            grid=(),
            in_specs=[VMEM, VMEM] + [ANY] * len(chunks),
            out_specs=VMEM,
            scratch_shapes=phi + [pltpu.VMEM((elements * rows, vectors), jnp.float32)] * 2 + sems,
        ),
        out_shape=jax.ShapeDtypeStruct((devices, ROWS, far), jnp.float32),
        name="applied",
    )(ids, rows_in, cap, *got)
    returned = lax.all_to_all(back, both, split_axis=0, concat_axis=0, tiled=True)
    galerkin = pl.pallas_call(
        functools.partial(galerkin_kernel, chunks, groups, per_pair),
        grid_spec=pltpu.PrefetchScalarGridSpec(
            num_scalar_prefetch=1,
            grid=(elements,),
            in_specs=[pl.BlockSpec((elements, ECELLS), lambda e, i: (0, 0))] + [ANY] * len(chunks),
            out_specs=pl.BlockSpec((1, rows, rows), lambda e, i: (e, 0, 0)),
            scratch_shapes=phi + sems,
        ),
        out_shape=jax.ShapeDtypeStruct((elements, rows, rows), jnp.float32),
        name="galerkin",
    )(ids, cap, *got)
    out = whole(
        functools.partial(sum_kernel, per_pair),
        (groups, ROWS, near),
        target,
        returned,
        scratch=scratch,
        prefetch=1,
        name="sum_octants",
    )
    out = lax.all_to_all(out, "eight", split_axis=0, concat_axis=0, tiled=True)
    coarse_out = whole(coarse_out_kernel, coarse_in.shape, out, name="coarse_out")
    return (galerkin, coarse_out)


def solution(mesh):
    in_specs = (
        P("wide", "eight", None),
        P("wide", None),
        P("wide"),
        P("wide", None),
        P(("wide", "eight"), None),
        P(("wide", "eight"), None, None),
    )
    out_specs = (P(("wide", "eight"), None, None), P(("wide", "eight"), None, None))
    return jax.shard_map(body, mesh=mesh, in_specs=in_specs, out_specs=out_specs, check_vma=False)
```

```python
import functools

import jax
import jax.numpy as jnp
from jax import lax
from jax.experimental import pallas as pl
from jax.experimental.pallas import tpu as pltpu
from jax.sharding import PartitionSpec as P

SIDE = 16
PASSES = 6
ECELLS = 512
LANES = 128
ROWS = 8
HALF = SIDE // 2
TILES = SIDE * SIDE * SIDE // LANES
PAIR = SIDE * SIDE // LANES

ANY = pl.BlockSpec(memory_space=pltpu.HBM)
VMEM = pl.BlockSpec(memory_space=pltpu.VMEM)
SMEM = pl.BlockSpec(memory_space=pltpu.SMEM)


def hat(i):
    return min(i + 0.5, SIDE - 0.5 - i) / HALF


def stencil_table(cond, w_ref):
    cells = cond.shape[1]
    at = lax.broadcasted_iota(jnp.int32, cond.shape, 1)
    diagonal = jnp.zeros_like(cond)
    links = []
    for stride in (SIDE * SIDE, SIDE, 1):
        position = (at // stride) % SIDE
        for toward in (-1, 1):
            beside = pltpu.roll(cond, (-toward * stride) % cells, 1)
            inside = (position + toward >= 0) & (position + toward < SIDE)
            face = 0.5 * (cond + jnp.where(inside, beside, cond))
            diagonal = diagonal + face
            links.append(jnp.where(inside, face, 0.0))
    upper = 2.0 * jnp.max(diagonal, axis=1, keepdims=True)
    twice = 2.0 / (0.4375 * upper)
    table = [(diagonal - 0.5625 * upper) * twice] + [link * twice for link in links]
    for i, values in enumerate(table):
        for t in range(TILES):
            w_ref[i, t] = values[:, t * LANES : (t + 1) * LANES]


def filter_kernel(first_slot, groups, target_ref, counts_ref, sv_ref, cond_ref, send_ref, w_ref, y_ref, out_ref, sems):
    n = pl.program_id(0)
    last = pl.num_programs(0) - 1
    rows = groups * ROWS
    lane = lax.broadcasted_iota(jnp.int32, (ROWS, LANES), 1)
    low_row = lane < SIDE
    high_row = lane >= LANES - SIDE

    @pl.when(n == 0)
    def _():
        stencil_table(cond_ref[...], w_ref)

    def weight(k, t):
        return w_ref[k, t, pl.ds(n, ROWS, 0), :]

    start = sv_ref[0].astype(jnp.float32)
    for g in range(groups):
        y_ref[0, g] = start[first_slot + g * ROWS : first_slot + (g + 1) * ROWS, :]

    squares = [jnp.zeros((ROWS, LANES), jnp.float32) for _ in range(groups)]
    for sweep in range(PASSES):
        src, dst, old = sweep % 3, (sweep + 1) % 3, (sweep + 2) % 3

        def tile(g, a, d):
            t = a * PAIR + d
            return y_ref[src, g, :, t * LANES : (t + 1) * LANES]

        window = [[None] + [[tile(g, a, d) for d in range(PAIR)] for a in range(1)] for g in range(groups)]
        for a in range(SIDE):
            ups = []
            for g in range(groups):
                below, here = window[g]
                above = [tile(g, a + 1, d) for d in range(PAIR)] if a + 1 < SIDE else None
                ups.append((below, here, above))
                window[g] = [here, above]
            back = [[pltpu.roll(u[1][d], SIDE, 1) for d in range(PAIR)] for u in ups]
            fore = [[pltpu.roll(u[1][d], LANES - SIDE, 1) for d in range(PAIR)] for u in ups]
            for d in range(PAIR):
                t = a * PAIR + d
                w = [weight(k, t) for k in range(7)]
                for g in range(groups):
                    below, here, above = ups[g]
                    value = w[0] * here[d]
                    if below is not None:
                        value = value - w[1] * below[d]
                    if above is not None:
                        value = value - w[2] * above[d]
                    lower = back[g][d] if d == 0 else jnp.where(low_row, back[g][d - 1], back[g][d])
                    upper = fore[g][d] if d == PAIR - 1 else jnp.where(high_row, fore[g][d + 1], fore[g][d])
                    value = value - w[3] * lower
                    value = value - w[4] * upper
                    value = value - w[5] * pltpu.roll(here[d], 1, 1)
                    value = value - w[6] * pltpu.roll(here[d], LANES - 1, 1)
                    if sweep == 0:
                        value = 0.5 * value
                    else:
                        value = value - y_ref[old, g, :, t * LANES : (t + 1) * LANES]
                    y_ref[dst, g, :, t * LANES : (t + 1) * LANES] = value
                    if sweep == PASSES - 1:
                        squares[g] = squares[g] + value * value
    final = PASSES % 3

    slot = lax.rem(n, 2)

    def copy_out(step_slot, piece, o):
        return pltpu.make_async_copy(out_ref.at[step_slot, o], send_ref.at[piece], sems.at[step_slot, o])

    @pl.when(n >= 2)
    def _():
        for o in range(8):
            copy_out(slot, 0, o).wait()

    column = lax.rem(lax.div(lane, SIDE), HALF)
    across = (lax.rem(lane, SIDE)).astype(jnp.float32)
    hat_c = jnp.minimum(across + 0.5, SIDE - 0.5 - across) / HALF
    even = lax.rem(lax.div(lane, HALF), 2) == 0
    bumps = []
    for d in range(PAIR):
        along = (column + d * HALF).astype(jnp.float32)
        bumps.append(hat_c * (jnp.minimum(along + 0.5, SIDE - 0.5 - along) / HALF))
    base = lax.axis_index("eight") * sv_ref.shape[1] + first_slot
    for g in range(groups):
        mean = jnp.sum(squares[g], axis=1, keepdims=True) / (TILES * LANES)
        row = lax.broadcasted_iota(jnp.int32, (ROWS, 1), 0) + (base + g * ROWS)
        scale = lax.rsqrt(mean + 1e-05) * (row < counts_ref[n]).astype(jnp.float32)
        for d in range(PAIR):
            weight_d = scale * bumps[d]
            for dx in range(2):
                for p in range(HALF // 2):
                    pair = []
                    for h in range(2):
                        a = dx * HALF + h * (HALF // 2) + p
                        t = a * PAIR + d
                        pair.append(y_ref[final, g, :, t * LANES : (t + 1) * LANES] * (weight_d * hat(a)))
                    near = jnp.where(even, pair[0], pltpu.roll(pair[1], HALF, 1))
                    far = jnp.where(even, pltpu.roll(pair[0], LANES - HALF, 1), pair[1])
                    for dz, value in enumerate((near, far)):
                        out_ref[slot, dx * 4 + d * 2 + dz, g * ROWS : (g + 1) * ROWS, p * LANES : (p + 1) * LANES] = value
    for o in range(8):
        copy_out(slot, target_ref[n * 8 + o], o).start()

    @pl.when(n == last)
    def _():
        for o in range(8):
            copy_out(1 - slot, 0, o).wait()
        for o in range(8):
            copy_out(slot, 0, o).wait()


def filter_call(first_slot, groups, target, counts, start_vectors, conductance):
    hoods, width, cells = start_vectors.shape
    rows = groups * ROWS
    return pl.pallas_call(
        functools.partial(filter_kernel, first_slot, groups),
        grid_spec=pltpu.PrefetchScalarGridSpec(
            num_scalar_prefetch=2,
            grid=(hoods,),
            in_specs=[
                pl.BlockSpec((1, width, cells), lambda n, t, c: (n, 0, 0)),
                pl.BlockSpec((hoods, cells), lambda n, t, c: (0, 0)),
            ],
            out_specs=ANY,
            scratch_shapes=[
                pltpu.VMEM((7, TILES, hoods, LANES), jnp.float32),
                pltpu.VMEM((3, groups, ROWS, cells), jnp.float32),
                pltpu.VMEM((2, 8, rows, ECELLS), jnp.float32),
                pltpu.SemaphoreType.DMA((2, 8)),
            ],
        ),
        out_shape=jax.ShapeDtypeStruct((hoods * 8, rows, ECELLS), jnp.float32),
        name="filter%d" % first_slot,
    )(target, counts, start_vectors, conductance)


def pack(blocks):
    if len(blocks) % 2:
        blocks = blocks + [jnp.zeros_like(blocks[0])]
    return [jnp.concatenate(blocks[i : i + 2], axis=1) for i in range(0, len(blocks), 2)]


def half(tile, k):
    vectors = LANES // 2
    return tile[:, (k % 2) * vectors : (k % 2 + 1) * vectors]


def packed_width(blocks):
    return (blocks + 1) // 2 * LANES


def sum_kernel(per_pair, source_ref, in_ref, after_ref, out_ref, rows_ref):
    del after_ref
    groups = out_ref.shape[0]
    hoods, width, _ = rows_ref.shape
    owned = hoods // groups
    bits = width // ROWS
    rows_ref[...] = jnp.zeros_like(rows_ref)

    def gather(d, carry):
        for i in range(per_pair):
            n = source_ref[d * per_pair + i]
            for r in range(bits):
                k = i * bits + r
                rows_ref[n, r * ROWS : (r + 1) * ROWS, :] += half(in_ref[d, :, k // 2 * LANES : (k // 2 + 1) * LANES], k)
        return carry

    lax.fori_loop(0, in_ref.shape[0], gather, 0)
    for e in range(groups):
        blocks = [
            rows_ref[e * owned + n, r * ROWS : (r + 1) * ROWS, :] for n in range(owned) for r in range(bits)
        ]
        for i, tile in enumerate(pack(blocks)):
            out_ref[e, :, i * LANES : (i + 1) * LANES] = tile


def coarse_out_kernel(in_ref, out_ref):
    groups = in_ref.shape[0]
    owned, _, slots = out_ref.shape
    bits = slots // groups // ROWS
    for n in range(owned):
        rows = []
        for e in range(groups):
            for r in range(bits):
                k = n * bits + r
                rows.append(half(in_ref[e, :, k // 2 * LANES : (k // 2 + 1) * LANES], k))
        out_ref[n] = jnp.transpose(jnp.concatenate(rows, axis=0))


def split(x):
    high = x.astype(jnp.bfloat16)
    return high, (x - high.astype(jnp.float32)).astype(jnp.bfloat16)


def product(x, y, dims):
    xh, xl = x
    yh, yl = y
    dot = functools.partial(lax.dot_general, dimension_numbers=(dims, ((), ())), preferred_element_type=jnp.float32)
    return dot(xh, yh) + (dot(xh, yl) + dot(xl, yh))


def start_gather(chunks, groups, per_pair, e, from_ref, got_refs, phi_ref, sems):
    width = sum(count for _, count in chunks) * ROWS
    for o in range(8):
        base = from_ref[e * 8 + o]
        for g in range(groups):
            q = base + g * per_pair
            row = (e * 8 + o) * groups * width + g * width
            for k, (first, count) in enumerate(chunks):
                rows = count * ROWS
                pltpu.make_async_copy(
                    got_refs[k].at[pl.ds(pl.multiple_of(q * rows, ROWS), rows)],
                    phi_ref.at[pl.ds(row + first, rows)],
                    sems.at[e],
                ).start()


def wait_gather(e, rows, got_refs, phi_ref, sems):
    pltpu.make_async_copy(
        got_refs[-1].at[pl.ds(0, rows)], phi_ref.at[pl.ds(pl.multiple_of(e * rows, ROWS), rows)], sems.at[e]
    ).wait()


def applied_kernel(chunks, groups, per_pair, from_ref, hood_ref, key_ref, all_ref, cap_ref, *refs):
    got_refs = refs[: len(chunks)]
    out_ref, phi_ref, r_ref, applied_ref, sems, r_sems = refs[len(chunks) :]
    width = sum(count for _, count in chunks) * ROWS
    bits = width // ROWS
    slots = groups * width
    rows = 8 * slots
    elements = cap_ref.shape[0]
    for e in range(elements):
        for o in range(8):
            k = e * 8 + o
            pltpu.make_async_copy(all_ref.at[hood_ref[k]], r_ref.at[k], r_sems.at[e]).start()
        start_gather(chunks, groups, per_pair, e, from_ref, got_refs, phi_ref, sems)
    for e in range(elements):
        pltpu.make_async_copy(all_ref.at[pl.ds(0, 8)], r_ref.at[pl.ds(e * 8, 8)], r_sems.at[e]).wait()
        wait_gather(e, rows, got_refs, phi_ref, sems)
        phi = split(phi_ref[e * rows : (e + 1) * rows, :])
        sums = jnp.zeros((r_ref.shape[1], ECELLS), jnp.float32)
        for o in range(8):
            r = split(r_ref[e * 8 + o, :, :slots])
            sums = sums + product(r, [x[o * slots : (o + 1) * slots] for x in phi], ((1,), (0,)))
        sums = sums * cap_ref[e : e + 1, :]
        applied_ref[e * rows : (e + 1) * rows, :] = product(phi, split(sums), ((1,), (1,)))

    def back(w, carry):
        keys = [key_ref[w * per_pair + i] * slots for i in range(per_pair)]
        for g in range(groups):
            blocks = []
            for i in range(per_pair):
                for r in range(bits):
                    row = pl.multiple_of(keys[i] + (g * width + r * ROWS), ROWS)
                    blocks.append(applied_ref[pl.ds(row, ROWS), :])
            for i, tile in enumerate(pack(blocks)):
                out_ref[w * groups + g, :, i * LANES : (i + 1) * LANES] = tile
        return carry

    lax.fori_loop(0, out_ref.shape[0] // groups, back, 0)


def galerkin_kernel(chunks, groups, per_pair, from_ref, cap_ref, *refs):
    got_refs = refs[: len(chunks)]
    out_ref, phi_ref, sems = refs[len(chunks) :]
    width = sum(count for _, count in chunks) * ROWS
    rows = 8 * groups * width
    e = pl.program_id(0)

    @pl.when(e == 0)
    def _():
        for i in range(cap_ref.shape[0]):
            start_gather(chunks, groups, per_pair, i, from_ref, got_refs, phi_ref, sems)

    wait_gather(e, rows, got_refs, phi_ref, sems)
    phi = phi_ref[pl.ds(pl.multiple_of(e * rows, ROWS), rows), :]
    weighted = phi * cap_ref[pl.ds(e, 1), :]
    out_ref[0] = product(split(weighted), split(phi), ((1,), (1,)))


CHUNKS = ((0, 1), (8, 2))


def exchange_steps(wide, groups):
    steps = []
    for axis, size in (("wide", wide), ("eight", groups)):
        distance = size // 2
        while distance:
            steps.append((axis, size, distance))
            distance //= 2
    return steps


def gather_all(x, steps):
    for axis, size, distance in steps:
        there = lax.ppermute(x, axis, [(i, i ^ distance) for i in range(size)])
        x = jnp.concatenate([x, there], axis=0)
    return x


def block_of(steps, wide_at, eight_at):
    at = {"wide": wide_at ^ lax.axis_index("wide"), "eight": eight_at ^ lax.axis_index("eight")}
    block = 0
    for k, (axis, _, distance) in enumerate(steps):
        block = block + jnp.where(at[axis] & distance, 1 << k, 0)
    return block


def body(start_vectors, conductance, counts, element_of, capacity, coarse_in):
    groups = lax.axis_size("eight")
    wide = lax.axis_size("wide")
    devices = wide * groups
    hoods, width, cells = start_vectors.shape
    owned = hoods // groups
    elements = capacity.shape[0]
    pieces = hoods * 8
    per_pair = pieces // devices
    slots, vectors = coarse_in.shape[1:]
    bits = width // ROWS
    chunks = CHUNKS
    both = ("wide", "eight")
    ints = jnp.int32

    owner = (element_of // elements).reshape(-1)
    order = jnp.arange(pieces, dtype=ints)
    earlier = (owner[:, None] == owner[None, :]) & (order[None, :] < order[:, None])
    target = owner * per_pair + jnp.sum(earlier.astype(ints), axis=1)

    got = []
    held = (coarse_in, element_of, capacity, target)
    for at, count in chunks:
        send = filter_call(at, count, target, counts, start_vectors, conductance)
        held, send = lax.optimization_barrier((held, send))
        send = send.reshape(devices, per_pair, count * ROWS, ECELLS)
        arrived = lax.all_to_all(send, both, split_axis=0, concat_axis=0, tiled=True)
        got.append(arrived.reshape(pieces * count * ROWS, ECELLS))
    coarse_in, element_of, capacity, late_target = held

    steps = exchange_steps(wide, groups)
    own = lax.dynamic_slice_in_dim(element_of, lax.axis_index("eight") * owned, owned, axis=0)
    margin = jnp.zeros((owned, vectors, LANES - slots), jnp.float32).at[:, 0, :8].set(own.astype(jnp.float32))
    every = gather_all(jnp.concatenate([jnp.swapaxes(coarse_in, 1, 2), margin], axis=2), steps)

    wide_at = jnp.arange(wide, dtype=ints)[:, None]
    eight_at = jnp.arange(groups, dtype=ints)[None, :]
    block = block_of(steps, wide_at, eight_at)
    incidence = every[:, 0, slots : slots + 8].reshape(devices, owned * 8)[block.reshape(-1)]
    incidence = incidence.astype(ints).reshape(wide, pieces)
    me = lax.axis_index("wide") * groups + lax.axis_index("eight")
    mine = incidence // elements == me
    before = (order[:, None] < order[None, :]).astype(jnp.float32)
    rank = jnp.dot(mine.astype(jnp.float32), before).astype(ints)
    key = incidence % elements * 8 + order[None, :] % 8
    hood = (block[:, :, None] * owned + jnp.arange(owned, dtype=ints)).reshape(wide, hoods)
    hood = jnp.broadcast_to(hood[:, :, None], (wide, hoods, 8)).reshape(wide, pieces)
    first = wide_at * (groups * per_pair) + rank
    chosen = mine[None] & (key[None] == jnp.arange(elements * 8, dtype=ints)[:, None, None])
    from_at = jnp.sum(jnp.where(chosen, first[None], 0), axis=(1, 2))
    hood_at = jnp.sum(jnp.where(chosen, hood[None], 0), axis=(1, 2))
    placed = mine[:, None, :] & (rank[:, None, :] == jnp.arange(per_pair, dtype=ints)[None, :, None])
    key_at = jnp.sum(jnp.where(placed, key[:, None, :], 0), axis=2).reshape(-1)
    hit = late_target[None, :] == order[:, None]
    source = jnp.sum(jnp.where(hit, order[None, :] // 8, 0), axis=1)

    near = packed_width(owned * bits)
    far = packed_width(per_pair * bits)
    cap = capacity.reshape(elements, 2, HALF // 2, HALF, HALF).transpose(0, 2, 3, 1, 4).reshape(elements, ECELLS) / ECELLS
    rows = 8 * slots
    phi = [pltpu.VMEM((elements * rows, ECELLS), jnp.float32)]
    sems = [pltpu.SemaphoreType.DMA((elements,))]
    back = pl.pallas_call(
        functools.partial(applied_kernel, chunks, groups, per_pair),
        grid_spec=pltpu.PrefetchScalarGridSpec(
            num_scalar_prefetch=3,
            grid=(),
            in_specs=[ANY, VMEM] + [ANY] * len(chunks),
            out_specs=VMEM,
            scratch_shapes=phi
            + [
                pltpu.VMEM((elements * 8, vectors, LANES), jnp.float32),
                pltpu.VMEM((elements * rows, vectors), jnp.float32),
            ]
            + sems * 2,
        ),
        out_shape=jax.ShapeDtypeStruct((devices, ROWS, far), jnp.float32),
        name="applied",
    )(from_at, hood_at, key_at, every, cap, *got)
    returned = lax.all_to_all(back, both, split_axis=0, concat_axis=0, tiled=True)
    galerkin = pl.pallas_call(
        functools.partial(galerkin_kernel, chunks, groups, per_pair),
        grid_spec=pltpu.PrefetchScalarGridSpec(
            num_scalar_prefetch=1,
            grid=(elements,),
            in_specs=[pl.BlockSpec((elements, ECELLS), lambda e, i: (0, 0))] + [ANY] * len(chunks),
            out_specs=pl.BlockSpec((1, rows, rows), lambda e, i: (e, 0, 0)),
            scratch_shapes=phi + sems,
        ),
        out_shape=jax.ShapeDtypeStruct((elements, rows, rows), jnp.float32),
        name="galerkin",
    )(from_at, cap, *got)
    out = pl.pallas_call(
        functools.partial(sum_kernel, per_pair),
        grid_spec=pltpu.PrefetchScalarGridSpec(
            num_scalar_prefetch=1,
            grid=(),
            in_specs=[VMEM, ANY],
            out_specs=VMEM,
            scratch_shapes=[pltpu.VMEM((hoods, width, vectors), jnp.float32)],
        ),
        out_shape=jax.ShapeDtypeStruct((groups, ROWS, near), jnp.float32),
        name="sum_octants",
    )(source, returned, galerkin)
    out = lax.all_to_all(out, "eight", split_axis=0, concat_axis=0, tiled=True)
    coarse_out = pl.pallas_call(
        coarse_out_kernel,
        in_specs=[VMEM],
        out_specs=VMEM,
        out_shape=jax.ShapeDtypeStruct((owned, vectors, slots), jnp.float32),
        name="coarse_out",
    )(out)
    return (galerkin, jnp.swapaxes(coarse_out, 1, 2))


def solution(mesh):
    in_specs = (
        P("wide", "eight", None),
        P("wide", None),
        P("wide"),
        P("wide", None),
        P(("wide", "eight"), None),
        P(("wide", "eight"), None, None),
    )
    out_specs = (P(("wide", "eight"), None, None), P(("wide", "eight"), None, None))
    return jax.shard_map(body, mesh=mesh, in_specs=in_specs, out_specs=out_specs, check_vma=False)
```

```python
import functools

import jax
import jax.numpy as jnp
from jax import lax
from jax.experimental import pallas as pl
from jax.experimental.pallas import tpu as pltpu
from jax.sharding import PartitionSpec as P

SIDE = 16
PASSES = 6
ECELLS = 512
LANES = 128
ROWS = 8
HALF = SIDE // 2
TILES = SIDE * SIDE * SIDE // LANES
PAIR = SIDE * SIDE // LANES

ANY = pl.BlockSpec(memory_space=pltpu.HBM)
VMEM = pl.BlockSpec(memory_space=pltpu.VMEM)
SMEM = pl.BlockSpec(memory_space=pltpu.SMEM)


def hat(i):
    return min(i + 0.5, SIDE - 0.5 - i) / HALF


def stencil_table(cond, w_ref):
    cells = cond.shape[1]
    at = lax.broadcasted_iota(jnp.int32, cond.shape, 1)
    diagonal = jnp.zeros_like(cond)
    links = []
    for stride in (SIDE * SIDE, SIDE, 1):
        position = (at // stride) % SIDE
        for toward in (-1, 1):
            beside = pltpu.roll(cond, (-toward * stride) % cells, 1)
            inside = (position + toward >= 0) & (position + toward < SIDE)
            face = 0.5 * (cond + jnp.where(inside, beside, cond))
            diagonal = diagonal + face
            links.append(jnp.where(inside, face, 0.0))
    upper = 2.0 * jnp.max(diagonal, axis=1, keepdims=True)
    twice = 2.0 / (0.4375 * upper)
    table = [(diagonal - 0.5625 * upper) * twice] + [link * twice for link in links]
    for i, values in enumerate(table):
        for t in range(TILES):
            w_ref[i, t] = values[:, t * LANES : (t + 1) * LANES]


def filter_kernel(first_slot, groups, per_pair, extra, *refs):
    target_ref, counts_ref, source_ref, sv_ref, cond_ref = refs[:5]
    extra_refs, (send_ref, w_ref, y_ref, out_ref, sems, more_ref, more_sem) = refs[5:-7], refs[-7:]
    n = pl.program_id(0)
    last = pl.num_programs(0) - 1
    rows = groups * ROWS
    lane = lax.broadcasted_iota(jnp.int32, (ROWS, LANES), 1)
    low_row = lane < SIDE
    high_row = lane >= LANES - SIDE

    @pl.when(n == 0)
    def _():
        stencil_table(cond_ref[...], w_ref)

    def weight(k, t):
        return w_ref[k, t, pl.ds(n, ROWS, 0), :]

    start = sv_ref[0].astype(jnp.float32)
    for g in range(groups):
        y_ref[0, g] = start[first_slot + g * ROWS : first_slot + (g + 1) * ROWS, :]

    squares = [jnp.zeros((ROWS, LANES), jnp.float32) for _ in range(groups)]
    for sweep in range(PASSES):
        src, dst, old = sweep % 3, (sweep + 1) % 3, (sweep + 2) % 3

        def tile(g, a, d):
            t = a * PAIR + d
            return y_ref[src, g, :, t * LANES : (t + 1) * LANES]

        window = [[None] + [[tile(g, a, d) for d in range(PAIR)] for a in range(1)] for g in range(groups)]
        for a in range(SIDE):
            ups = []
            for g in range(groups):
                below, here = window[g]
                above = [tile(g, a + 1, d) for d in range(PAIR)] if a + 1 < SIDE else None
                ups.append((below, here, above))
                window[g] = [here, above]
            back = [[pltpu.roll(u[1][d], SIDE, 1) for d in range(PAIR)] for u in ups]
            fore = [[pltpu.roll(u[1][d], LANES - SIDE, 1) for d in range(PAIR)] for u in ups]
            for d in range(PAIR):
                t = a * PAIR + d
                w = [weight(k, t) for k in range(7)]
                for g in range(groups):
                    below, here, above = ups[g]
                    value = w[0] * here[d]
                    if below is not None:
                        value = value - w[1] * below[d]
                    if above is not None:
                        value = value - w[2] * above[d]
                    lower = back[g][d] if d == 0 else jnp.where(low_row, back[g][d - 1], back[g][d])
                    upper = fore[g][d] if d == PAIR - 1 else jnp.where(high_row, fore[g][d + 1], fore[g][d])
                    value = value - w[3] * lower
                    value = value - w[4] * upper
                    value = value - w[5] * pltpu.roll(here[d], 1, 1)
                    value = value - w[6] * pltpu.roll(here[d], LANES - 1, 1)
                    if sweep == 0:
                        value = 0.5 * value
                    else:
                        value = value - y_ref[old, g, :, t * LANES : (t + 1) * LANES]
                    y_ref[dst, g, :, t * LANES : (t + 1) * LANES] = value
                    if sweep == PASSES - 1:
                        squares[g] = squares[g] + value * value
    final = PASSES % 3

    slot = lax.rem(n, 2)

    def copy_out(step_slot, piece, o):
        at = pl.multiple_of(lax.rem(piece, per_pair) * 4 * rows, ROWS)
        place = send_ref.at[lax.div(piece, per_pair), pl.ds(at, 4 * rows)]
        return pltpu.make_async_copy(out_ref.at[step_slot, o], place, sems.at[step_slot, o])

    @pl.when(n >= 2)
    def _():
        for o in range(8):
            copy_out(slot, 0, o).wait()

    column = lax.rem(lax.div(lane, SIDE), HALF)
    across = (lax.rem(lane, SIDE)).astype(jnp.float32)
    hat_c = jnp.minimum(across + 0.5, SIDE - 0.5 - across) / HALF
    even = lax.rem(lax.div(lane, HALF), 2) == 0
    bumps = []
    for d in range(PAIR):
        along = (column + d * HALF).astype(jnp.float32)
        bumps.append(hat_c * (jnp.minimum(along + 0.5, SIDE - 0.5 - along) / HALF))
    base = lax.axis_index("eight") * sv_ref.shape[1] + first_slot
    for g in range(groups):
        mean = jnp.sum(squares[g], axis=1, keepdims=True) / (TILES * LANES)
        row = lax.broadcasted_iota(jnp.int32, (ROWS, 1), 0) + (base + g * ROWS)
        scale = lax.rsqrt(mean + 1e-05) * (row < counts_ref[n]).astype(jnp.float32)
        for d in range(PAIR):
            weight_d = scale * bumps[d]
            for dx in range(2):
                for p in range(HALF // 2):
                    pair = []
                    for h in range(2):
                        a = dx * HALF + h * (HALF // 2) + p
                        t = a * PAIR + d
                        pair.append(y_ref[final, g, :, t * LANES : (t + 1) * LANES] * (weight_d * hat(a)))
                    near = jnp.where(even, pair[0], pltpu.roll(pair[1], HALF, 1))
                    far = jnp.where(even, pltpu.roll(pair[0], LANES - HALF, 1), pair[1])
                    for dz, value in enumerate((near, far)):
                        at = p * rows + g * ROWS
                        out_ref[slot, dx * 4 + d * 2 + dz, at : at + ROWS, :] = value
    for o in range(8):
        copy_out(slot, target_ref[n * 8 + o], o).start()

    @pl.when(n == last)
    def _():
        extra(per_pair, source_ref, *extra_refs, more_ref)
        base = per_pair * 4 * rows
        more = pltpu.make_async_copy(more_ref, send_ref.at[:, pl.ds(base, more_ref.shape[1])], more_sem)
        more.start()
        more.wait()
        for o in range(8):
            copy_out(1 - slot, 0, o).wait()
        for o in range(8):
            copy_out(slot, 0, o).wait()


def filter_call(first_slot, groups, devices, target, counts, source, start_vectors, conductance, extra, more_rows, more=()):
    hoods, width, cells = start_vectors.shape
    rows = groups * ROWS
    per_pair = hoods * 8 // devices
    return pl.pallas_call(
        functools.partial(filter_kernel, first_slot, groups, per_pair, extra),
        grid_spec=pltpu.PrefetchScalarGridSpec(
            num_scalar_prefetch=3,
            grid=(hoods,),
            in_specs=[
                pl.BlockSpec((1, width, cells), lambda n, *_: (n, 0, 0)),
                pl.BlockSpec((hoods, cells), lambda n, *_: (0, 0)),
            ]
            + [pl.BlockSpec(x.shape, lambda n, *_, k=x.ndim: (0,) * k) for x in more],
            out_specs=ANY,
            scratch_shapes=[
                pltpu.VMEM((7, TILES, hoods, LANES), jnp.float32),
                pltpu.VMEM((3, groups, ROWS, cells), jnp.float32),
                pltpu.VMEM((2, 8, 4 * rows, LANES), jnp.float32),
                pltpu.SemaphoreType.DMA((2, 8)),
                pltpu.VMEM((devices, more_rows, LANES), jnp.float32),
                pltpu.SemaphoreType.DMA,
            ],
        ),
        out_shape=jax.ShapeDtypeStruct((devices, per_pair * 4 * rows + more_rows, LANES), jnp.float32),
        name="filter%d" % first_slot,
    )(target, counts, source, start_vectors, conductance, *more)


def pack(blocks):
    if len(blocks) % 2:
        blocks = blocks + [jnp.zeros_like(blocks[0])]
    return [jnp.concatenate(blocks[i : i + 2], axis=1) for i in range(0, len(blocks), 2)]


def half(tile, k):
    vectors = LANES // 2
    return tile[:, (k % 2) * vectors : (k % 2 + 1) * vectors]


def hypercube_bits(block, size):
    place, distance = 0, size // 2
    while distance:
        place += distance * (block & 1)
        block >>= 1
        distance //= 2
    return place


def hypercube_step(x, axis, size, distance):
    there = lax.ppermute(x, axis, [(i, i ^ distance) for i in range(size)])
    return jnp.concatenate([x, there], axis=0)


def packed_rows(blocks):
    return (blocks + 1) // 2 * ROWS


def send_keys(elements, per_pair, source_ref, out_ref):
    lane = lax.broadcasted_iota(jnp.int32, (ROWS, LANES), 1)

    def place(d, carry):
        tile = jnp.zeros((ROWS, LANES), jnp.int32)
        for i in range(per_pair):
            key = lax.rem(source_ref[d * per_pair + i], elements * 8)
            tile = jnp.where(lane == i, key, tile)
        out_ref[d] = tile.astype(jnp.float32)
        return carry

    lax.fori_loop(0, out_ref.shape[0], place, 0)


def send_rows(per_pair, source_ref, in_ref, out_ref):
    hoods, vectors, slots = in_ref.shape
    fill = functools.partial(fill_rows, per_pair, source_ref, in_ref, out_ref)
    pl.run_scoped(fill, pltpu.VMEM((hoods, slots, vectors), jnp.float32))


def fill_rows(per_pair, source_ref, in_ref, out_ref, rows_ref):
    groups = lax.axis_size("eight")
    hoods, _, slots = in_ref.shape
    owned = hoods // groups
    width = slots // groups
    bits = width // ROWS
    me = lax.axis_index("eight")
    for block in range(groups):
        e = me ^ hypercube_bits(block, groups)
        for n in range(owned):
            rows_ref[e * owned + n] = jnp.transpose(in_ref[block * owned + n])

    def place(d, carry):
        blocks = []
        for i in range(per_pair):
            n = source_ref[d * per_pair + i]
            for r in range(bits):
                at = pl.multiple_of(me * width + r * ROWS, ROWS)
                blocks.append(rows_ref[n, pl.ds(at, ROWS), :])
        for k, tile in enumerate(pack(blocks)):
            out_ref[d, k * ROWS : (k + 1) * ROWS, :] = tile
        return carry

    lax.fori_loop(0, out_ref.shape[0], place, 0)


def sum_kernel(per_pair, source_ref, in_ref, after_ref, out_ref, rows_ref):
    del after_ref
    groups = out_ref.shape[0]
    hoods, width, _ = rows_ref.shape
    owned = hoods // groups
    bits = width // ROWS
    rows_ref[...] = jnp.zeros_like(rows_ref)

    def gather(d, carry):
        for i in range(per_pair):
            n = source_ref[d * per_pair + i]
            for r in range(bits):
                k = i * bits + r
                rows_ref[n, r * ROWS : (r + 1) * ROWS, :] += half(in_ref[d, k // 2 * ROWS : (k // 2 + 1) * ROWS, :], k)
        return carry

    lax.fori_loop(0, in_ref.shape[0], gather, 0)
    for e in range(groups):
        blocks = [
            rows_ref[e * owned + n, r * ROWS : (r + 1) * ROWS, :] for n in range(owned) for r in range(bits)
        ]
        for i, tile in enumerate(pack(blocks)):
            out_ref[e, i * ROWS : (i + 1) * ROWS, :] = tile


def coarse_out_kernel(in_ref, out_ref):
    groups = in_ref.shape[0]
    owned, _, slots = out_ref.shape
    bits = slots // groups // ROWS
    for n in range(owned):
        rows = []
        for e in range(groups):
            for r in range(bits):
                k = n * bits + r
                rows.append(half(in_ref[e, k // 2 * ROWS : (k // 2 + 1) * ROWS, :], k))
        out_ref[n] = jnp.transpose(jnp.concatenate(rows, axis=0))


def split(x):
    high = x.astype(jnp.bfloat16)
    return high, (x - high.astype(jnp.float32)).astype(jnp.bfloat16)


def product(x, y, dims):
    xh, xl = x
    yh, yl = y
    dot = functools.partial(lax.dot_general, dimension_numbers=(dims, ((), ())), preferred_element_type=jnp.float32)
    return dot(xh, yh) + (dot(xh, yl) + dot(xl, yh))


def start_gather(chunks, groups, per_pair, e, from_ref, got_refs, phi_ref, sems):
    width = sum(count for _, count in chunks) * ROWS
    for o in range(8):
        source = from_ref[e * 8 + o]
        device = lax.div(source, per_pair) * groups
        i = lax.rem(source, per_pair)
        for g in range(groups):
            row = (e * 8 + o) * groups * width + g * width
            for k, (first, count) in enumerate(chunks):
                pltpu.make_async_copy(
                    got_refs[k].at[device + g, pl.ds(i * 4, 4)],
                    phi_ref.at[:, pl.ds(row + first, count * ROWS)],
                    sems.at[e],
                ).start()


def wait_gather(e, rows, phi_ref, sems):
    part = phi_ref.at[:, pl.ds(pl.multiple_of(e * rows, ROWS), rows)]
    pltpu.make_async_copy(part, part, sems.at[e]).wait()


def basis_of(e, rows, phi_ref):
    at = pl.ds(pl.multiple_of(e * rows, ROWS), rows)
    return jnp.concatenate([phi_ref[p, at, :] for p in range(4)], axis=1)


def dot(x, y, x_dim, y_dim):
    return lax.dot_general(x, y, (((x_dim,), (y_dim,)), ((), ())), preferred_element_type=jnp.float32)


def applied_kernel(chunks, groups, per_pair, from_ref, key_ref, cap_ref, *refs):
    got_refs = refs[: len(chunks)]
    out_ref, phi_ref, rows_ref, r_ref, applied_ref, sems, rows_sem = refs[len(chunks) :]
    width = sum(count for _, count in chunks) * ROWS
    bits = width // ROWS
    slots = groups * width
    rows = 8 * slots
    elements = cap_ref.shape[0]
    wide = out_ref.shape[0] // groups
    per_block = rows_ref.shape[2] // ROWS
    coarse = pltpu.make_async_copy(got_refs[-1].at[:, pl.ds(per_pair * 4, rows_ref.shape[1])], rows_ref, rows_sem)
    coarse.start()
    for e in range(elements):
        start_gather(chunks, groups, per_pair, e, from_ref, got_refs, phi_ref, sems)
    coarse.wait()

    def place(w, carry):
        for i in range(per_pair):
            key = key_ref[w * per_pair + i] * slots
            for g in range(groups):
                for r in range(bits):
                    k = i * bits + r
                    t = k // 2
                    at = t % per_block * ROWS
                    row = pl.multiple_of(key + (g * width + r * ROWS), ROWS)
                    r_ref[pl.ds(row, ROWS), :] = half(rows_ref[w * groups + g, t // per_block, at : at + ROWS, :], k)
        return carry

    lax.fori_loop(0, wide, place, 0)
    for e in range(elements):
        r = jnp.concatenate(split(jnp.transpose(r_ref[e * rows : (e + 1) * rows, :])), axis=0)
        vectors = r.shape[0] // 2
        wait_gather(e, rows, phi_ref, sems)
        high, low = split(basis_of(e, rows, phi_ref))
        both = dot(r, high, 1, 0)
        sums = both[:vectors] + (both[vectors:] + dot(r[:vectors], low, 1, 0))
        sums = jnp.concatenate(split(sums * cap_ref[e : e + 1, :]), axis=0)
        both = dot(high, sums, 1, 1)
        applied = both[:, :vectors] + (both[:, vectors:] + dot(low, sums[:vectors], 1, 1))
        applied_ref[e * rows : (e + 1) * rows, :] = applied

    def back(w, carry):
        keys = [key_ref[w * per_pair + i] * slots for i in range(per_pair)]
        for g in range(groups):
            blocks = []
            for i in range(per_pair):
                for r in range(bits):
                    row = pl.multiple_of(keys[i] + (g * width + r * ROWS), ROWS)
                    blocks.append(applied_ref[pl.ds(row, ROWS), :])
            for i, tile in enumerate(pack(blocks)):
                out_ref[w * groups + g, i * ROWS : (i + 1) * ROWS, :] = tile
        return carry

    lax.fori_loop(0, wide, back, 0)


def galerkin_kernel(chunks, groups, per_pair, from_ref, cap_ref, *refs):
    got_refs = refs[: len(chunks)]
    out_ref, phi_ref, sems = refs[len(chunks) :]
    width = sum(count for _, count in chunks) * ROWS
    rows = 8 * groups * width
    e = pl.program_id(0)

    @pl.when(e == 0)
    def _():
        for i in range(cap_ref.shape[0]):
            start_gather(chunks, groups, per_pair, i, from_ref, got_refs, phi_ref, sems)

    wait_gather(e, rows, phi_ref, sems)
    phi = basis_of(e, rows, phi_ref)
    out_ref[0] = product(split(phi * cap_ref[pl.ds(e, 1), :]), split(phi), ((1,), (1,)))


CHUNKS = ((0, 1), (8, 2))


def body(start_vectors, conductance, counts, element_of, capacity, coarse_in):
    groups = lax.axis_size("eight")
    wide = lax.axis_size("wide")
    devices = wide * groups
    hoods, width, cells = start_vectors.shape
    owned = hoods // groups
    elements = capacity.shape[0]
    pieces = hoods * 8
    per_pair = pieces // devices
    slots, vectors = coarse_in.shape[1:]
    bits = width // ROWS
    chunks = CHUNKS
    both = ("wide", "eight")
    ints = jnp.int32

    owner = (element_of // elements).reshape(-1)
    order = jnp.arange(pieces, dtype=ints)
    earlier = (owner[:, None] == owner[None, :]) & (order[None, :] < order[:, None])
    target = owner * per_pair + jnp.sum(earlier.astype(ints), axis=1)

    hit = target[None, :] == order[:, None]
    local = (element_of % elements * 8 + jnp.arange(8, dtype=ints)[None, :]).reshape(-1)
    keys = jnp.sum(jnp.where(hit, local[None, :], 0), axis=1)
    source = jnp.sum(jnp.where(hit, order[None, :] // 8, 0), axis=1)
    far = packed_rows(per_pair * bits)
    near = packed_rows(owned * bits)

    def exchange(send, rows):
        arrived = lax.all_to_all(send, both, split_axis=0, concat_axis=0, tiled=True)
        return arrived.reshape(devices, -1, rows, LANES)

    filtered = functools.partial(filter_call, devices=devices, target=target, counts=counts)
    filtered = functools.partial(filtered, start_vectors=start_vectors, conductance=conductance)
    distance = groups // 2
    coarse = hypercube_step(jnp.swapaxes(coarse_in, 1, 2), "eight", groups, distance)
    (at, count), (late, more) = chunks
    send = filtered(at, count, source=keys, extra=functools.partial(send_keys, elements), more_rows=ROWS)
    coarse, send = lax.optimization_barrier((coarse, send))
    first = exchange(send, count * ROWS)
    while distance > 1:
        distance //= 2
        coarse = hypercube_step(coarse, "eight", groups, distance)
    send = filtered(late, more, source=source, extra=send_rows, more_rows=far, more=(coarse,))
    second = exchange(send, more * ROWS)
    got = [first, second]

    key_at = first[:: groups, 4 * per_pair, 0, :per_pair].astype(ints).reshape(-1)
    chosen = key_at[None, :] == jnp.arange(elements * 8, dtype=ints)[:, None]
    from_at = jnp.sum(jnp.where(chosen, jnp.arange(wide * per_pair, dtype=ints)[None, :], 0), axis=1)

    cap = capacity.reshape(elements, 2, HALF // 2, HALF, HALF).transpose(0, 2, 3, 1, 4).reshape(elements, ECELLS) / ECELLS
    rows = 8 * slots
    phi = [pltpu.VMEM((4, elements * rows, LANES), jnp.float32)]
    sems = [pltpu.SemaphoreType.DMA((elements,))]
    back = pl.pallas_call(
        functools.partial(applied_kernel, chunks, groups, per_pair),
        grid_spec=pltpu.PrefetchScalarGridSpec(
            num_scalar_prefetch=2,
            grid=(),
            in_specs=[VMEM] + [ANY] * len(chunks),
            out_specs=VMEM,
            scratch_shapes=phi
            + [
                pltpu.VMEM((devices, far // (more * ROWS), more * ROWS, LANES), jnp.float32),
                pltpu.VMEM((elements * rows, vectors), jnp.float32),
                pltpu.VMEM((elements * rows, vectors), jnp.float32),
            ]
            + sems
            + [pltpu.SemaphoreType.DMA],
        ),
        out_shape=jax.ShapeDtypeStruct((devices, far, LANES), jnp.float32),
        name="applied",
    )(from_at, key_at, cap, *got)
    returned = lax.all_to_all(back, both, split_axis=0, concat_axis=0, tiled=True)
    galerkin = pl.pallas_call(
        functools.partial(galerkin_kernel, chunks, groups, per_pair),
        grid_spec=pltpu.PrefetchScalarGridSpec(
            num_scalar_prefetch=1,
            grid=(elements,),
            in_specs=[pl.BlockSpec((elements, ECELLS), lambda e, i: (0, 0))] + [ANY] * len(chunks),
            out_specs=pl.BlockSpec((1, rows, rows), lambda e, i: (e, 0, 0)),
            scratch_shapes=phi + sems,
        ),
        out_shape=jax.ShapeDtypeStruct((elements, rows, rows), jnp.float32),
        name="galerkin",
    )(from_at, cap, *got)
    out = pl.pallas_call(
        functools.partial(sum_kernel, per_pair),
        grid_spec=pltpu.PrefetchScalarGridSpec(
            num_scalar_prefetch=1,
            grid=(),
            in_specs=[VMEM, ANY],
            out_specs=VMEM,
            scratch_shapes=[pltpu.VMEM((hoods, width, vectors), jnp.float32)],
        ),
        out_shape=jax.ShapeDtypeStruct((groups, near, LANES), jnp.float32),
        name="sum_octants",
    )(source, returned, galerkin)
    out = lax.all_to_all(out, "eight", split_axis=0, concat_axis=0, tiled=True)
    coarse_out = pl.pallas_call(
        coarse_out_kernel,
        in_specs=[VMEM],
        out_specs=VMEM,
        out_shape=jax.ShapeDtypeStruct((owned, vectors, slots), jnp.float32),
        name="coarse_out",
    )(out)
    return (galerkin, jnp.swapaxes(coarse_out, 1, 2))


def solution(mesh):
    in_specs = (
        P("wide", "eight", None),
        P("wide", None),
        P("wide"),
        P("wide", None),
        P(("wide", "eight"), None),
        P(("wide", "eight"), None, None),
    )
    out_specs = (P(("wide", "eight"), None, None), P(("wide", "eight"), None, None))
    return jax.shard_map(body, mesh=mesh, in_specs=in_specs, out_specs=out_specs, check_vma=False)
```

```python
import functools

import jax
import jax.numpy as jnp
from jax import lax
from jax.experimental import pallas as pl
from jax.experimental.pallas import tpu as pltpu
from jax.sharding import PartitionSpec as P

SIDE = 16
PASSES = 6
ECELLS = 512
LANES = 128
ROWS = 8
HALF = SIDE // 2
TILES = SIDE * SIDE * SIDE // LANES
PAIR = SIDE * SIDE // LANES

ANY = pl.BlockSpec(memory_space=pltpu.HBM)
VMEM = pl.BlockSpec(memory_space=pltpu.VMEM)
SCOPED = pltpu.CompilerParams(vmem_limit_bytes=28 << 20)


def hat(i):
    return min(i + 0.5, SIDE - 0.5 - i) / HALF


def stencil_table(cond, w_ref):
    cells = cond.shape[1]
    at = lax.broadcasted_iota(jnp.int32, cond.shape, 1)
    diagonal = jnp.zeros_like(cond)
    links = []
    for stride in (SIDE * SIDE, SIDE, 1):
        position = (at // stride) % SIDE
        for toward in (-1, 1):
            beside = pltpu.roll(cond, (-toward * stride) % cells, 1)
            inside = (position + toward >= 0) & (position + toward < SIDE)
            face = 0.5 * (cond + jnp.where(inside, beside, cond))
            diagonal = diagonal + face
            links.append(jnp.where(inside, face, 0.0))
    upper = 2.0 * jnp.max(diagonal, axis=1, keepdims=True)
    twice = 2.0 / (0.4375 * upper)
    table = [(diagonal - 0.5625 * upper) * twice] + [link * twice for link in links]
    for i, values in enumerate(table):
        for t in range(TILES):
            w_ref[i, t] = values[:, t * LANES : (t + 1) * LANES]


def filter_kernel(first_slot, groups, per_pair, elements, extra, *refs):
    element_ref, counts_ref, sv_ref, cond_ref = refs[:4]
    extra_refs, refs = refs[4:-9], refs[-9:]
    send_ref, w_ref, y_ref, out_ref, sems, more_ref, more_sem, used_ref, note_ref = refs
    n = pl.program_id(0)
    devices = send_ref.shape[0]

    last = pl.num_programs(0) - 1
    rows = groups * ROWS
    lane = lax.broadcasted_iota(jnp.int32, (ROWS, LANES), 1)
    low_row = lane < SIDE
    high_row = lane >= LANES - SIDE

    @pl.when(n == 0)
    def _():
        stencil_table(cond_ref[...], w_ref)
        for d in range(devices):
            used_ref[d] = 0

    targets = []
    for o in range(8):
        element = element_ref[n, o]
        owner = lax.div(element, elements)
        i = used_ref[owner]
        used_ref[owner] = i + 1
        note_ref[owner * per_pair + i] = (n * elements + lax.rem(element, elements)) * 8 + o
        targets.append((owner, i))

    def weight(k, t):
        return w_ref[k, t, pl.ds(n, ROWS, 0), :]

    start = sv_ref[0].astype(jnp.float32)
    for g in range(groups):
        y_ref[0, g] = start[first_slot + g * ROWS : first_slot + (g + 1) * ROWS, :]

    squares = [jnp.zeros((ROWS, LANES), jnp.float32) for _ in range(groups)]
    for sweep in range(PASSES):
        src, dst, old = sweep % 3, (sweep + 1) % 3, (sweep + 2) % 3

        def tile(g, a, d):
            t = a * PAIR + d
            return y_ref[src, g, :, t * LANES : (t + 1) * LANES]

        window = [[None] + [[tile(g, a, d) for d in range(PAIR)] for a in range(1)] for g in range(groups)]
        for a in range(SIDE):
            ups = []
            for g in range(groups):
                below, here = window[g]
                above = [tile(g, a + 1, d) for d in range(PAIR)] if a + 1 < SIDE else None
                ups.append((below, here, above))
                window[g] = [here, above]
            back = [[pltpu.roll(u[1][d], SIDE, 1) for d in range(PAIR)] for u in ups]
            fore = [[pltpu.roll(u[1][d], LANES - SIDE, 1) for d in range(PAIR)] for u in ups]
            for d in range(PAIR):
                t = a * PAIR + d
                w = [weight(k, t) for k in range(7)]
                for g in range(groups):
                    below, here, above = ups[g]
                    value = w[0] * here[d]
                    if below is not None:
                        value = value - w[1] * below[d]
                    if above is not None:
                        value = value - w[2] * above[d]
                    lower = back[g][d] if d == 0 else jnp.where(low_row, back[g][d - 1], back[g][d])
                    upper = fore[g][d] if d == PAIR - 1 else jnp.where(high_row, fore[g][d + 1], fore[g][d])
                    value = value - w[3] * lower
                    value = value - w[4] * upper
                    value = value - w[5] * pltpu.roll(here[d], 1, 1)
                    value = value - w[6] * pltpu.roll(here[d], LANES - 1, 1)
                    if sweep == 0:
                        value = 0.5 * value
                    else:
                        value = value - y_ref[old, g, :, t * LANES : (t + 1) * LANES]
                    y_ref[dst, g, :, t * LANES : (t + 1) * LANES] = value
                    if sweep == PASSES - 1:
                        squares[g] = squares[g] + value * value
    final = PASSES % 3

    slot = lax.rem(n, 2)

    def copy_out(step_slot, target, o):
        at = pl.multiple_of(target[1] * (4 * rows), ROWS)
        place = send_ref.at[target[0], pl.ds(at, 4 * rows)]
        return pltpu.make_async_copy(out_ref.at[step_slot, o], place, sems.at[step_slot, o])

    @pl.when(n >= 2)
    def _():
        for o in range(8):
            copy_out(slot, (0, 0), o).wait()

    column = lax.rem(lax.div(lane, SIDE), HALF)
    across = (lax.rem(lane, SIDE)).astype(jnp.float32)
    hat_c = jnp.minimum(across + 0.5, SIDE - 0.5 - across) / HALF
    even = lax.rem(lax.div(lane, HALF), 2) == 0
    bumps = []
    for d in range(PAIR):
        along = (column + d * HALF).astype(jnp.float32)
        bumps.append(hat_c * (jnp.minimum(along + 0.5, SIDE - 0.5 - along) / HALF))
    base = lax.axis_index("eight") * sv_ref.shape[1] + first_slot
    for g in range(groups):
        mean = jnp.sum(squares[g], axis=1, keepdims=True) / (TILES * LANES)
        row = lax.broadcasted_iota(jnp.int32, (ROWS, 1), 0) + (base + g * ROWS)
        scale = lax.rsqrt(mean + 1e-05) * (row < counts_ref[n]).astype(jnp.float32)
        for d in range(PAIR):
            weight_d = scale * bumps[d]
            for dx in range(2):
                for p in range(HALF // 2):
                    pair = []
                    for h in range(2):
                        a = dx * HALF + h * (HALF // 2) + p
                        t = a * PAIR + d
                        pair.append(y_ref[final, g, :, t * LANES : (t + 1) * LANES] * (weight_d * hat(a)))
                    near = jnp.where(even, pair[0], pltpu.roll(pair[1], HALF, 1))
                    far = jnp.where(even, pltpu.roll(pair[0], LANES - HALF, 1), pair[1])
                    for dz, value in enumerate((near, far)):
                        at = p * rows + g * ROWS
                        out_ref[slot, dx * 4 + d * 2 + dz, at : at + ROWS, :] = value
    for o in range(8):
        copy_out(slot, targets[o], o).start()

    @pl.when(n == last)
    def _():
        extra(per_pair, elements, note_ref, *extra_refs, more_ref)
        base = per_pair * 4 * rows
        more = pltpu.make_async_copy(more_ref, send_ref.at[:, pl.ds(base, more_ref.shape[1])], more_sem)
        more.start()
        more.wait()
        for o in range(8):
            copy_out(1 - slot, (0, 0), o).wait()
        for o in range(8):
            copy_out(slot, (0, 0), o).wait()


def filter_call(first_slot, groups, devices, elements, element_of, counts, start_vectors, conductance, extra, more_rows, more=()):
    hoods, width, cells = start_vectors.shape
    rows = groups * ROWS
    per_pair = hoods * 8 // devices
    return pl.pallas_call(
        functools.partial(filter_kernel, first_slot, groups, per_pair, elements, extra),
        grid_spec=pltpu.PrefetchScalarGridSpec(
            num_scalar_prefetch=2,
            grid=(hoods,),
            in_specs=[
                pl.BlockSpec((1, width, cells), lambda n, *_: (n, 0, 0)),
                pl.BlockSpec((hoods, cells), lambda n, *_: (0, 0)),
            ]
            + [pl.BlockSpec(x.shape, lambda n, *_, k=x.ndim: (0,) * k) for x in more],
            out_specs=ANY,
            scratch_shapes=[
                pltpu.VMEM((7, TILES, hoods, LANES), jnp.float32),
                pltpu.VMEM((3, groups, ROWS, cells), jnp.float32),
                pltpu.VMEM((2, 8, 4 * rows, LANES), jnp.float32),
                pltpu.SemaphoreType.DMA((2, 8)),
                pltpu.VMEM((devices, more_rows, LANES), jnp.float32),
                pltpu.SemaphoreType.DMA,
                pltpu.SMEM((devices,), jnp.int32),
                pltpu.SMEM((hoods * 8,), jnp.int32),
            ],
        ),
        out_shape=pltpu.HBM((devices, per_pair * 4 * rows + more_rows, LANES), jnp.float32),
        compiler_params=SCOPED,
        name="filter%d" % first_slot,
    )(element_of, counts, start_vectors, conductance, *more)


def pack(pieces):
    if len(pieces) % 2:
        pieces = pieces + [[jnp.zeros_like(x) for x in pieces[0]]]
    return [
        jnp.concatenate(pair, axis=1) for i in range(0, len(pieces), 2) for pair in zip(pieces[i], pieces[i + 1])
    ]


def part(i, r, bits):
    t = (i // 2 * bits + r) * ROWS
    return slice(t, t + ROWS), slice(i % 2 * (LANES // 2), (i % 2 + 1) * (LANES // 2))


def hypercube_bits(block, size):
    place, distance = 0, size // 2
    while distance:
        place += distance * (block & 1)
        block >>= 1
        distance //= 2
    return place


def hypercube_step(x, axis, size, distance):
    there = lax.ppermute(x, axis, [(i, i ^ distance) for i in range(size)])
    return jnp.concatenate([x, there], axis=0)


def packed_rows(pieces, bits):
    return (pieces + 1) // 2 * bits * ROWS


def send_keys(per_pair, elements, note_ref, out_ref):
    lane = lax.broadcasted_iota(jnp.int32, (ROWS, LANES), 1)

    def place(d, carry):
        tile = jnp.zeros((ROWS, LANES), jnp.int32)
        for i in range(per_pair):
            tile = jnp.where(lane == i, lax.rem(note_ref[d * per_pair + i], elements * 8), tile)
        out_ref[d] = tile.astype(jnp.float32)
        return carry

    lax.fori_loop(0, out_ref.shape[0], place, 0)


def send_rows(per_pair, elements, note_ref, in_ref, out_ref):
    hoods, vectors, slots = in_ref.shape
    fill = functools.partial(fill_rows, per_pair, elements, note_ref, in_ref, out_ref)
    pl.run_scoped(fill, pltpu.VMEM((hoods, slots, vectors), jnp.float32))


def fill_rows(per_pair, elements, note_ref, in_ref, out_ref, rows_ref):
    groups = lax.axis_size("eight")
    hoods, _, slots = in_ref.shape
    owned = hoods // groups
    width = slots // groups
    me = lax.axis_index("eight")
    for block in range(groups):
        e = me ^ hypercube_bits(block, groups)
        for n in range(owned):
            rows_ref[e * owned + n] = jnp.transpose(in_ref[block * owned + n])

    def place(d, carry):
        pieces = []
        for i in range(per_pair):
            n = lax.div(note_ref[d * per_pair + i], elements * 8)
            at = [pl.multiple_of(me * width + r, ROWS) for r in range(0, width, ROWS)]
            pieces.append([rows_ref[n, pl.ds(x, ROWS), :] for x in at])
        for k, tile in enumerate(pack(pieces)):
            out_ref[d, k * ROWS : (k + 1) * ROWS, :] = tile
        return carry

    lax.fori_loop(0, out_ref.shape[0], place, 0)


def sum_kernel(per_pair, bits, target_ref, in_ref, after_ref, *out_refs):
    del after_ref
    groups = len(out_refs)
    owned = target_ref.shape[0] // 8 // groups
    me = lax.axis_index("eight")
    left = lax.broadcasted_iota(jnp.int32, (ROWS, LANES), 1) < LANES // 2
    for distance, out_ref in enumerate(out_refs):
        pieces = []
        for k in range(owned):
            n = (me ^ distance) * owned + k
            sums = [jnp.zeros((ROWS, LANES), jnp.float32)] * bits
            for o in range(8):
                target = target_ref[n * 8 + o]
                i = lax.rem(target, per_pair)
                first = lax.div(i, 2) * bits
                wanted = left == (lax.rem(i, 2) == 0)
                for r in range(bits):
                    at = pl.multiple_of((first + r) * ROWS, ROWS)
                    sums[r] += jnp.where(wanted, in_ref[lax.div(target, per_pair), pl.ds(at, ROWS), :], 0.0)
            pieces.append([x[:, : LANES // 2] + x[:, LANES // 2 :] for x in sums])
        for i, tile in enumerate(pack(pieces)):
            out_ref[i * ROWS : (i + 1) * ROWS, :] = tile


def coarse_out_kernel(bits, *refs):
    in_refs, out_ref, rows_ref = refs[:-2], refs[-2], refs[-1]
    me = lax.axis_index("eight")
    for distance, in_ref in enumerate(in_refs):
        for n in range(out_ref.shape[0]):
            for r in range(bits):
                at = pl.multiple_of((me ^ distance) * (bits * ROWS) + r * ROWS, ROWS)
                rows, lanes = part(n, r, bits)
                rows_ref[n, pl.ds(at, ROWS), :] = in_ref[rows, lanes]
    for n in range(out_ref.shape[0]):
        out_ref[n] = jnp.transpose(rows_ref[n])


def split(x):
    high = x.astype(jnp.bfloat16)
    return high, (x - high.astype(jnp.float32)).astype(jnp.bfloat16)


def product(x, y, dims):
    xh, xl = x
    yh, yl = y
    dot = functools.partial(lax.dot_general, dimension_numbers=(dims, ((), ())), preferred_element_type=jnp.float32)
    return dot(xh, yh) + (dot(xh, yl) + dot(xl, yh))


def basis_of(e, chunks, groups, per_pair, from_ref, got_refs):
    columns = [[] for _ in range(4)]
    for o in range(8):
        source = from_ref[e * 8 + o]
        device = lax.div(source, per_pair) * groups
        i = lax.rem(source, per_pair)
        for g in range(groups):
            for k, (_, count) in enumerate(chunks):
                rows = count * ROWS
                for p in range(4):
                    at = pl.multiple_of(i * (4 * rows) + p * rows, ROWS)
                    columns[p].append(got_refs[k][device + g, pl.ds(at, rows), :])
    return jnp.concatenate([jnp.concatenate(x, axis=0) for x in columns], axis=1)


def dot(x, y, x_dim, y_dim):
    return lax.dot_general(x, y, (((x_dim,), (y_dim,)), ((), ())), preferred_element_type=jnp.float32)


def applied_kernel(chunks, groups, per_pair, from_ref, key_ref, cap_ref, *refs):
    got_refs = refs[: len(chunks)]
    out_ref, r_ref, applied_ref = refs[len(chunks) :]
    width = sum(count for _, count in chunks) * ROWS
    bits = width // ROWS
    slots = groups * width
    rows = 8 * slots
    elements = cap_ref.shape[0]
    wide = out_ref.shape[0] // groups
    base = per_pair * 4 * chunks[-1][1] * ROWS

    def place(w, carry):
        for i in range(per_pair):
            key = key_ref[w * per_pair + i] * slots
            for g in range(groups):
                for r in range(bits):
                    at, lanes = part(i, r, bits)
                    row = pl.multiple_of(key + (g * width + r * ROWS), ROWS)
                    r_ref[pl.ds(row, ROWS), :] = got_refs[-1][w * groups + g, base + at.start : base + at.stop, lanes]
        return carry

    lax.fori_loop(0, wide, place, 0)
    for e in range(elements):
        r = jnp.concatenate(split(jnp.transpose(r_ref[e * rows : (e + 1) * rows, :])), axis=0)
        vectors = r.shape[0] // 2
        high, low = split(basis_of(e, chunks, groups, per_pair, from_ref, got_refs))
        both = dot(r, high, 1, 0)
        sums = both[:vectors] + (both[vectors:] + dot(r[:vectors], low, 1, 0))
        sums = jnp.concatenate(split(sums * cap_ref[e : e + 1, :]), axis=0)
        both = dot(high, sums, 1, 1)
        applied = both[:, :vectors] + (both[:, vectors:] + dot(low, sums[:vectors], 1, 1))
        applied_ref[e * rows : (e + 1) * rows, :] = applied

    def back(w, carry):
        keys = [key_ref[w * per_pair + i] * slots for i in range(per_pair)]
        for g in range(groups):
            at = [g * width + r for r in range(0, width, ROWS)]
            pieces = [[applied_ref[pl.ds(pl.multiple_of(key + x, ROWS), ROWS), :] for x in at] for key in keys]
            for i, tile in enumerate(pack(pieces)):
                out_ref[w * groups + g, i * ROWS : (i + 1) * ROWS, :] = tile
        return carry

    lax.fori_loop(0, wide, back, 0)


def galerkin_kernel(chunks, groups, per_pair, from_ref, cap_ref, *refs):
    got_refs, out_ref = refs[:-1], refs[-1]
    e = pl.program_id(0)
    phi = basis_of(e, chunks, groups, per_pair, from_ref, got_refs)
    out_ref[0] = product(split(phi * cap_ref[pl.ds(e, 1), :]), split(phi), ((1,), (1,)))


CHUNKS = ((0, 1), (8, 2))


def body(start_vectors, conductance, counts, element_of, capacity, coarse_in):
    groups = lax.axis_size("eight")
    wide = lax.axis_size("wide")
    devices = wide * groups
    hoods, width, cells = start_vectors.shape
    owned = hoods // groups
    elements = capacity.shape[0]
    pieces = hoods * 8
    per_pair = pieces // devices
    slots, vectors = coarse_in.shape[1:]
    bits = width // ROWS
    chunks = CHUNKS
    both = ("wide", "eight")
    ints = jnp.int32

    far = packed_rows(per_pair, bits)
    in_vmem = functools.partial(pltpu.with_memory_space_constraint, memory_space=pltpu.VMEM)
    in_hbm = functools.partial(pltpu.with_memory_space_constraint, memory_space=pltpu.HBM)

    def exchange(send):
        return lax.all_to_all(send, both, split_axis=0, concat_axis=0, tiled=True)

    filtered = functools.partial(filter_call, devices=devices, elements=elements, element_of=element_of)
    filtered = functools.partial(filtered, counts=counts, start_vectors=in_hbm(start_vectors), conductance=in_hbm(conductance))
    distance = groups // 2
    coarse = hypercube_step(jnp.swapaxes(coarse_in, 1, 2), "eight", groups, distance)
    (at, count), (late, more) = chunks
    send = filtered(at, count, extra=send_keys, more_rows=ROWS)
    coarse, later_element_of, capacity, send = lax.optimization_barrier((coarse, element_of, capacity, send))
    first = exchange(send)
    while distance > 1:
        distance //= 2
        coarse = hypercube_step(coarse, "eight", groups, distance)
    send = filtered(late, more, extra=send_rows, more_rows=far, more=(coarse,))
    second = exchange(send)
    got = [in_vmem(first), in_vmem(second)]

    owner = (later_element_of // elements).reshape(-1)
    order = jnp.arange(pieces, dtype=ints)
    earlier = (owner[:, None] == owner[None, :]) & (order[None, :] < order[:, None])
    target = owner * per_pair + jnp.sum(earlier.astype(ints), axis=1)
    key_at = first[::groups, 4 * per_pair * count * ROWS, :per_pair].astype(ints).reshape(-1)
    chosen = key_at[None, :] == jnp.arange(elements * 8, dtype=ints)[:, None]
    from_at = jnp.sum(jnp.where(chosen, jnp.arange(wide * per_pair, dtype=ints)[None, :], 0), axis=1)

    cap = capacity.reshape(elements, 2, HALF // 2, HALF, HALF).transpose(0, 2, 3, 1, 4).reshape(elements, ECELLS) / ECELLS
    rows = 8 * slots
    back = pl.pallas_call(
        functools.partial(applied_kernel, chunks, groups, per_pair),
        grid_spec=pltpu.PrefetchScalarGridSpec(
            num_scalar_prefetch=2,
            grid=(),
            in_specs=[VMEM] * (1 + len(chunks)),
            out_specs=VMEM,
            scratch_shapes=[pltpu.VMEM((elements * rows, vectors), jnp.float32)] * 2,
        ),
        out_shape=pltpu.HBM((devices, far, LANES), jnp.float32),
        compiler_params=SCOPED,
        name="applied",
    )(from_at, key_at, cap, *got)
    returned = in_vmem(exchange(back))
    galerkin = pl.pallas_call(
        functools.partial(galerkin_kernel, chunks, groups, per_pair),
        grid_spec=pltpu.PrefetchScalarGridSpec(
            num_scalar_prefetch=1,
            grid=(elements,),
            in_specs=[pl.BlockSpec((elements, ECELLS), lambda e, i: (0, 0))] + [VMEM] * len(chunks),
            out_specs=pl.BlockSpec((1, rows, rows), lambda e, i: (e, 0, 0)),
        ),
        out_shape=pltpu.HBM((elements, rows, rows), jnp.float32),
        compiler_params=SCOPED,
        name="galerkin",
    )(from_at, cap, *got)
    near = packed_rows(owned, bits)
    outs = pl.pallas_call(
        functools.partial(sum_kernel, per_pair, bits),
        grid_spec=pltpu.PrefetchScalarGridSpec(
            num_scalar_prefetch=1,
            grid=(),
            in_specs=[VMEM, ANY],
            out_specs=[VMEM] * groups,
        ),
        out_shape=[jax.ShapeDtypeStruct((near, LANES), jnp.float32)] * groups,
        compiler_params=SCOPED,
        name="sum_octants",
    )(target, returned, in_hbm(galerkin))
    ends = [outs[0]]
    for distance in range(1, groups):
        ends.append(in_vmem(lax.ppermute(outs[distance], "eight", [(i, i ^ distance) for i in range(groups)])))
    coarse_out = pl.pallas_call(
        functools.partial(coarse_out_kernel, bits),
        in_specs=[VMEM] * groups,
        out_specs=VMEM,
        out_shape=jax.ShapeDtypeStruct((owned, vectors, slots), jnp.float32),
        scratch_shapes=[pltpu.VMEM((owned, slots, vectors), jnp.float32)],
        compiler_params=SCOPED,
        name="coarse_out",
    )(*ends)
    return (galerkin, jnp.swapaxes(coarse_out, 1, 2))


def solution(mesh):
    in_specs = (
        P("wide", "eight", None),
        P("wide", None),
        P("wide"),
        P("wide", None),
        P(("wide", "eight"), None),
        P(("wide", "eight"), None, None),
    )
    out_specs = (P(("wide", "eight"), None, None), P(("wide", "eight"), None, None))
    return jax.shard_map(body, mesh=mesh, in_specs=in_specs, out_specs=out_specs, check_vma=False)
```
